32 devices in a mesh: ep: 8 (over z, x), rep: 4 (over y, core).
Axes of the slice: x: 2, y: 2, z: 4, core: 2. Of those that a mesh axis runs over, the one named last changes fastest.
Arguments:
- context: bfloat16 [2048, 2048], P(('ep', 'rep')), may hold values from -6 to 6
- residual: bfloat16 [2048, 2048], P(('ep', 'rep')), may hold values from -125 to 125
- out_proj: bfloat16 [2048, 2048], replicated, may hold values from -0.125 to 0.125
- attn_gain: bfloat16 [2048], replicated, may hold values from 0.25 to 1.75
- router: bfloat16 [2048, 64], replicated, may hold values from -18 to 18
- expert_ids: int32 [2048, 8], P(('ep', 'rep')), may hold values from 0 to 63, as said below
- gate_weight: bfloat16 [64, 2048, 1024], P('ep', None, 'rep'), may hold values from -0.125 to 0.125
- up_weight: bfloat16 [64, 2048, 1024], P('ep', None, 'rep'), may hold values from -0.125 to 0.125
- down_weight: bfloat16 [64, 2048, 1024], P('ep', None, 'rep'), may hold values from -1.5 to 1.5
- final_gain: bfloat16 [2048], replicated, may hold values from 0.25 to 1.75
Outputs:
- layer_out: bfloat16 [2048, 2048], P(('ep', 'rep'))
The draws below stay inside these ranges and needn't reach their ends.
Inputs may be any that keep to these rules, and one draw needn't show every extreme that they name: `expert_ids`: the rows of one device name exactly 32 distinct experts, each of them exactly 16 times. The entries of a row are distinct. Every expert is named by some row.
All inputs are finite; a program needn't handle non-finite values.
Results may differ from the reference program's by a relative error of at most 0.005.
Values may be sent and summed in bfloat16 or wider, within the bound.
A program may use at most 192 MiB of HBM per device.

```python
import jax
import jax.numpy as jnp
from jax import lax

D = 2048
FF = 1024
EXPERTS = 64
TOP = 8
ROW_DEV = 64
ROWS = 2048
CAP = 16
FQ = 256
N_EP = 8
N_REP = 4


def draw_router(key, part):
    router_draw = 0.6 * jnp.clip(jax.random.normal(jax.random.fold_in(key, 12), (D, EXPERTS), jnp.float32), -4.0, 4.0) * D ** (-0.5)
    return router_draw.astype(jnp.bfloat16)


def draw_residual(key, part):
    drawn_draw = jnp.clip(jax.random.normal(jax.random.fold_in(key, 21), (ROWS, D), jnp.float32), -4.0, 4.0)
    values = 0.7 * drawn_draw
    return values.astype(jnp.bfloat16)


def draw_expert_ids(key, part):
    device_total = ROWS // ROW_DEV
    circle = 4 * TOP
    ranking = jax.random.permutation(jax.random.fold_in(key, 31), EXPERTS).astype(jnp.int32)
    expert_range = jnp.arange(EXPERTS, dtype=jnp.int32)
    popular_rank = jnp.zeros((EXPERTS,), jnp.int32).at[ranking].set(expert_range)
    favour = jnp.where(popular_rank < EXPERTS // 8, 4096, jnp.where(popular_rank < 3 * EXPERTS // 8, 2048, 0)).astype(jnp.int32)

    def slot_permutation(slot_key):
        return jax.random.permutation(slot_key, TOP).astype(jnp.int32)

    def one_device(device_index):
        device_key = jax.random.fold_in(jax.random.fold_in(key, 32), device_index)
        jitter = jax.random.randint(jax.random.fold_in(device_key, 1), (EXPERTS,), 0, 4096, dtype=jnp.int32)
        first_forced = 2 * device_index % EXPERTS
        second_forced = (2 * device_index + 1) % EXPERTS
        forced = ((expert_range == first_forced) | (expert_range == second_forced)).astype(jnp.int32) * 65536
        scores = (jitter + favour + forced) * EXPERTS + expert_range
        _, chosen = lax.top_k(scores, circle)
        chosen = chosen.astype(jnp.int32)
        chosen = chosen[jax.random.permutation(jax.random.fold_in(device_key, 2), circle).astype(jnp.int32)]
        shifts = jax.random.randint(jax.random.fold_in(device_key, 3), (ROW_DEV // 4,), 0, circle, dtype=jnp.int32)
        row_number = jnp.arange(ROW_DEV, dtype=jnp.int32)
        starts = TOP * (row_number % 4) + shifts[row_number // 4]
        slot_order = jax.vmap(slot_permutation)(jax.random.split(jax.random.fold_in(device_key, 4), ROW_DEV))
        positions = (starts[:, None] + slot_order) % circle
        picked = chosen[positions]
        row_order = jax.random.permutation(jax.random.fold_in(device_key, 5), ROW_DEV).astype(jnp.int32)
        return picked[row_order]
    stacked = jax.vmap(one_device)(jnp.arange(device_total, dtype=jnp.int32))
    return stacked.reshape(ROWS, TOP).astype(jnp.int32)


def block_levels(key, dims, cuts, low, largest):
    gain, own = 1.0, jax.random.fold_in(key, 6)
    for position, blocks in cuts:
        draws = jnp.exp(jax.random.uniform(jax.random.fold_in(own, position), (blocks,), jnp.float32, low / len(cuts), largest / len(cuts)))
        gain = gain * jnp.repeat(draws, dims[position] // blocks).reshape([-1 if axis == position else 1 for axis in range(len(dims))])
    return gain


def normal_values(rng, shape, deviation, reach, shards=(), held_as=jnp.bfloat16):
    gain = block_levels(rng, shape, shards, -0.22, 0.18) if shards else 1.0
    values = jax.random.normal(rng, shape, jnp.float32) * deviation * gain
    return jnp.minimum(jnp.maximum(values, -reach), reach).astype(held_as)


def setup_inputs(seed: int = 0) -> dict:
    keys = jax.random.split(jax.random.key(seed), 11)
    return {
        "context": normal_values(keys[0], (ROWS, D), 1.0, 6.0, ((0, 32),)),
        "residual": draw_residual(jax.random.fold_in(keys[10], 71), 0),
        "out_proj": normal_values(keys[2], (D, D), D ** -0.5, 0.125),
        "attn_gain": jnp.clip(1.0 + 0.15 * jax.random.normal(keys[3], (D,), jnp.float32), 0.25, 1.75).astype(jnp.bfloat16),
        "router": draw_router(jax.random.fold_in(keys[10], 71), 0),
        "expert_ids": draw_expert_ids(jax.random.fold_in(keys[10], 71), 0),
        "gate_weight": normal_values(keys[6], (EXPERTS, D, FF), D ** -0.5, 0.125, ((0, 8), (2, 4))),
        "up_weight": normal_values(keys[7], (EXPERTS, D, FF), D ** -0.5, 0.125, ((0, 8), (2, 4))),
        "down_weight": normal_values(keys[8], (EXPERTS, D, FF), (max(FF // 64, 1)) ** -0.5, 1.5, ((0, 8), (2, 4))),
        "final_gain": jnp.clip(1.0 + 0.15 * jax.random.normal(keys[9], (D,), jnp.float32), 0.25, 1.75).astype(jnp.bfloat16),
    }


epsilon = 1e-05

def rms_scale(values, gain_vector):
    mean_square = lax.optimization_barrier(jnp.mean(values * values, axis=-1, keepdims=True))
    return values * lax.rsqrt(mean_square + epsilon) * gain_vector.astype(jnp.float32)

def reference(context, residual, out_proj, attn_gain, router, expert_ids, gate_weight, up_weight, down_weight, final_gain):
    devices = N_EP * N_REP
    pair_count = ROW_DEV * TOP
    attention = jnp.dot(context, out_proj, preferred_element_type=jnp.float32)
    mixed_stream = residual.astype(jnp.float32) + attention
    normed = rms_scale(mixed_stream, attn_gain).astype(jnp.bfloat16)
    logits = jnp.dot(normed, router, preferred_element_type=jnp.float32)
    probs = jax.nn.softmax(logits, axis=1)
    route_weight = jnp.take_along_axis(probs, expert_ids, axis=1)
    flat_ids = expert_ids.reshape(devices, pair_count)
    one_hot = (flat_ids[:, :, None] == jnp.arange(EXPERTS, dtype=jnp.int32)[None, None, :]).astype(jnp.int32)
    slot_rank = lax.optimization_barrier(jnp.sum(jnp.cumsum(one_hot, axis=1) * one_hot, axis=2)) - 1
    device_of = jnp.broadcast_to(jnp.arange(devices, dtype=jnp.int32)[:, None], (devices, pair_count))
    row_of = device_of * ROW_DEV + (jnp.arange(pair_count, dtype=jnp.int32) // TOP)[None, :]
    table = jnp.full((EXPERTS, devices, CAP), ROWS, jnp.int32).at[flat_ids, device_of, slot_rank].set(row_of)
    weight_table = jnp.zeros((EXPERTS, devices, CAP), jnp.float32).at[flat_ids, device_of, slot_rank].set(route_weight.reshape(devices, pair_count))
    padded = jnp.concatenate([normed, jnp.zeros((1, D), jnp.bfloat16)], axis=0)

    def one_expert(running, expert_index):
        row_index = table[expert_index].reshape(-1)
        batch_rows = padded[row_index]
        gate_all = gate_weight[expert_index]
        up_all = up_weight[expert_index]
        down_all = down_weight[expert_index]
        result = jnp.zeros((devices * CAP, D), jnp.float32)
        for quarter in range(N_REP):
            offset = quarter * FQ
            gate_proj = jnp.dot(batch_rows, gate_all[:, offset:offset + FQ], preferred_element_type=jnp.float32)
            up_proj = jnp.dot(batch_rows, up_all[:, offset:offset + FQ], preferred_element_type=jnp.float32)
            active = (jax.nn.silu(gate_proj) * up_proj).astype(jnp.bfloat16)
            part_sum = jnp.dot(active, down_all[:, offset:offset + FQ].T, preferred_element_type=jnp.float32)
            result = result + lax.optimization_barrier(part_sum.astype(jnp.bfloat16)).astype(jnp.float32)
        rounded = lax.optimization_barrier(result.astype(jnp.bfloat16)).astype(jnp.float32)
        contrib = weight_table[expert_index].reshape(-1, 1) * rounded
        return (running.at[row_index].add(contrib), None)
    start_sum = jnp.zeros((ROWS + 1, D), jnp.float32)
    expert_mix, _ = lax.scan(one_expert, start_sum, jnp.arange(EXPERTS, dtype=jnp.int32))
    total = mixed_stream + expert_mix[:ROWS]
    return rms_scale(total, final_gain).astype(jnp.bfloat16)
```

```python
import jax
import jax.numpy as jnp
from jax import lax
from jax.sharding import PartitionSpec as P

epsilon = 1e-05
capacity = 16


def rms_scale(values, gain_vector):
    mean_square = jnp.mean(values * values, axis=-1, keepdims=True)
    return values * lax.rsqrt(mean_square + epsilon) * gain_vector.astype(jnp.float32)


def front(context, residual, out_proj, attn_gain, router, expert_ids):
    expert_count = router.shape[1]
    attention = jnp.dot(context, out_proj, preferred_element_type=jnp.float32)
    mixed_stream = residual.astype(jnp.float32) + attention
    normed = rms_scale(mixed_stream, attn_gain).astype(jnp.bfloat16)
    logits = jnp.dot(normed, router, preferred_element_type=jnp.float32)
    probs = jax.nn.softmax(logits, axis=1)
    chosen = jnp.any(
        expert_ids[:, :, None] == jnp.arange(expert_count, dtype=jnp.int32)[None, None, :], axis=1
    )
    weights = jnp.where(chosen, probs, 0.0)
    return mixed_stream, normed, weights


def gathered(
    context, residual, out_proj, attn_gain, router, expert_ids,
    gate_weight, up_weight, down_weight, final_gain,
):
    row_count, model_width = context.shape
    local_experts = gate_weight.shape[0]
    owners = lax.axis_size("ep")
    sources = owners * lax.axis_size("rep")
    mixed_stream, normed, weights = front(
        context, residual, out_proj, attn_gain, router, expert_ids
    )
    high = weights.astype(jnp.bfloat16)
    low = (weights - high.astype(jnp.float32)).astype(jnp.bfloat16)
    block = jnp.concatenate([normed, high, low], axis=1)
    everyone = lax.all_gather(block, ("ep", "rep"), axis=0, tiled=False)
    rows = everyone[:, :, :model_width]
    first = model_width + lax.axis_index("ep") * local_experts
    high = lax.dynamic_slice_in_dim(everyone, first, local_experts, axis=2)
    low = lax.dynamic_slice_in_dim(everyone, first + weights.shape[1], local_experts, axis=2)
    local_weights = high.astype(jnp.float32) + low.astype(jnp.float32)
    mask = (local_weights > 0).astype(jnp.float32)
    earlier = (
        jnp.arange(row_count)[:, None] > jnp.arange(row_count)[None, :]
    ).astype(jnp.float32)
    rank = jnp.einsum("ij,sje->sie", earlier, mask)
    slots = jnp.arange(capacity, dtype=jnp.float32)
    placing = jnp.where(
        (rank[:, :, :, None] == slots) & (mask[:, :, :, None] > 0), 1.0, 0.0
    )
    slot_weight = jnp.sum(placing * local_weights[:, :, :, None], axis=1)
    placing = placing.astype(jnp.bfloat16).reshape(sources, row_count, local_experts * capacity)
    grouped = jnp.einsum(
        "sit,sid->std", placing, rows, preferred_element_type=jnp.float32
    ).astype(jnp.bfloat16)
    grouped = grouped.reshape(sources, local_experts, capacity, model_width)
    gate_proj = jnp.einsum(
        "serd,edw->serw", grouped, gate_weight, preferred_element_type=jnp.float32
    )
    up_proj = jnp.einsum("serd,edw->serw", grouped, up_weight, preferred_element_type=jnp.float32)
    active = (jax.nn.silu(gate_proj) * up_proj * slot_weight[..., None]).astype(jnp.bfloat16)
    part = jnp.einsum(
        "serw,edw->serd", active, down_weight, preferred_element_type=jnp.float32
    ).astype(jnp.bfloat16)
    part = part.reshape(sources, local_experts * capacity, model_width)
    share = jnp.einsum("sit,std->sid", placing, part, preferred_element_type=jnp.float32)
    share = share.astype(jnp.bfloat16).reshape(sources * row_count, model_width)
    expert_mix = lax.psum_scatter(share, ("ep", "rep"), scatter_dimension=0, tiled=True)
    total = mixed_stream + expert_mix.astype(jnp.float32)
    return rms_scale(total, final_gain).astype(jnp.bfloat16)


def solution(mesh):
    in_specs = (
        P(("ep", "rep"), None),
        P(("ep", "rep"), None),
        P(),
        P(),
        P(),
        P(("ep", "rep"), None),
        P("ep", None, "rep"),
        P("ep", None, "rep"),
        P("ep", None, "rep"),
        P(),
    )
    out_specs = P(("ep", "rep"), None)
    return jax.shard_map(
        gathered, mesh=mesh, in_specs=in_specs, out_specs=out_specs, check_vma=False
    )
```

```python
import jax
import jax.numpy as jnp
from jax import lax
from jax.experimental import pallas as pl
from jax.experimental.pallas import tpu as pltpu
from jax.sharding import PartitionSpec as P

epsilon = 1e-05
capacity = 16


def rms_scale(values, gain_vector):
    mean_square = jnp.mean(values * values, axis=-1, keepdims=True)
    return values * lax.rsqrt(mean_square + epsilon) * gain_vector.astype(jnp.float32)


def front(context, residual, out_proj, attn_gain, router, expert_ids):
    expert_count = router.shape[1]
    attention = jnp.dot(context, out_proj, preferred_element_type=jnp.float32)
    mixed_stream = residual.astype(jnp.float32) + attention
    normed = rms_scale(mixed_stream, attn_gain).astype(jnp.bfloat16)
    logits = jnp.dot(normed, router, preferred_element_type=jnp.float32)
    probs = jax.nn.softmax(logits, axis=1)
    chosen = jnp.any(
        expert_ids[:, :, None] == jnp.arange(expert_count, dtype=jnp.int32)[None, None, :], axis=1
    )
    weights = jnp.where(chosen, probs, 0.0)
    return mixed_stream, normed, weights


def gathered(
    context, residual, out_proj, attn_gain, router, expert_ids,
    gate_weight, up_weight, down_weight, final_gain,
):
    row_count, model_width = context.shape
    local_experts = gate_weight.shape[0]
    owners = lax.axis_size("ep")
    sources = owners * lax.axis_size("rep")
    mixed_stream, normed, weights = front(
        context, residual, out_proj, attn_gain, router, expert_ids
    )
    high = weights.astype(jnp.bfloat16)
    low = (weights - high.astype(jnp.float32)).astype(jnp.bfloat16)
    block = jnp.concatenate([normed, high, low], axis=1)
    everyone = lax.all_gather(block, ("ep", "rep"), axis=0, tiled=False)
    rows = everyone[:, :, :model_width]
    first = model_width + lax.axis_index("ep") * local_experts
    high = lax.dynamic_slice_in_dim(everyone, first, local_experts, axis=2)
    low = lax.dynamic_slice_in_dim(everyone, first + weights.shape[1], local_experts, axis=2)
    local_weights = high.astype(jnp.float32) + low.astype(jnp.float32)
    mask = (local_weights > 0).astype(jnp.float32)
    earlier = (
        jnp.arange(row_count)[:, None] > jnp.arange(row_count)[None, :]
    ).astype(jnp.float32)
    rank = jnp.einsum("ij,sje->sie", earlier, mask)
    slots = jnp.arange(capacity, dtype=jnp.float32)
    placing = jnp.where(
        (rank[:, :, :, None] == slots) & (mask[:, :, :, None] > 0), 1.0, 0.0
    )
    slot_weight = jnp.sum(placing * local_weights[:, :, :, None], axis=1)
    placing = placing.astype(jnp.bfloat16).reshape(sources, row_count, local_experts * capacity)
    grouped = jnp.einsum(
        "sit,sid->std", placing, rows, preferred_element_type=jnp.float32
    ).astype(jnp.bfloat16)
    grouped = grouped.reshape(sources, local_experts, capacity, model_width)
    gate_proj = jnp.einsum(
        "serd,edw->serw", grouped, gate_weight, preferred_element_type=jnp.float32
    )
    up_proj = jnp.einsum("serd,edw->serw", grouped, up_weight, preferred_element_type=jnp.float32)
    active = (jax.nn.silu(gate_proj) * up_proj * slot_weight[..., None]).astype(jnp.bfloat16)
    part = jnp.einsum(
        "serw,edw->serd", active, down_weight, preferred_element_type=jnp.float32
    ).astype(jnp.bfloat16)
    part = part.reshape(sources, local_experts * capacity, model_width)
    share = jnp.einsum("sit,std->sid", placing, part, preferred_element_type=jnp.float32)
    share = share.astype(jnp.bfloat16).reshape(sources * row_count, model_width)
    expert_mix = lax.psum_scatter(share, ("ep", "rep"), scatter_dimension=0, tiled=True)
    total = mixed_stream + expert_mix.astype(jnp.float32)
    return rms_scale(total, final_gain).astype(jnp.bfloat16)


MESH = pl.DeviceIdType.MESH
LINE = 4
OWN, FLIP_Y, FLIP_X, FLIP_BOTH = 0, 1, 2, 3


def box_kernel(
    block_ref, mixed_ref, gain_ref, gate_hbm, up_hbm, down_hbm, out_ref,
    rows, gate, up, down, grouped, placing, slot_weight,
    sibling_share, sibling_sum, share, first_x, first_y, second_x, second_y, column, last,
    weight_sem, send_sem, recv_sem,
):
    half = block_ref.shape[0] // 2
    width = mixed_ref.shape[1]
    extra = block_ref.shape[1] - width
    expert_count = extra // 2
    local = gate.shape[0]
    chunk = 2 * LINE * half
    slots = LINE * capacity
    tile = 512
    tiles = width // tile

    ep, rep = lax.axis_index("ep"), lax.axis_index("rep")
    z, x, y, core = ep // 2, ep % 2, rep // 2, rep % 2
    across_x = (z * 2 + (1 - x), rep)
    across_y = (ep, (1 - y) * 2 + core)
    sibling = (ep, y * 2 + (1 - core))

    def along_z(step):
        return (((z + step) % LINE) * 2 + x, rep)

    peers = [across_x, across_y, sibling] + [along_z(step) for step in (1, 2, 3)]
    barrier = pltpu.get_barrier_semaphore()
    for peer in peers:
        pl.semaphore_signal(barrier, inc=1, device_id=peer, device_id_type=MESH)
    weight_copies = [
        pltpu.make_async_copy(source, target, weight_sem.at[i])
        for i, (source, target) in enumerate(((gate_hbm, gate), (up_hbm, up), (down_hbm, down)))
    ]
    for copy in weight_copies:
        copy.start()
    pl.semaphore_wait(barrier, len(peers))

    started = []

    def send(source, target, device):
        index = len(started)
        copy = pltpu.make_async_remote_copy(
            src_ref=source, dst_ref=target, send_sem=send_sem.at[index],
            recv_sem=recv_sem.at[index], device_id=device, device_id_type=MESH,
        )
        copy.start()
        started.append(copy)
        return copy

    rows[0, OWN, 0, 0] = block_ref[:half]
    rows[0, OWN, 1, 0] = block_ref[half:]
    order = (0, 1, 3, 2)
    from_z = {
        k: send(rows.at[0, OWN, :, 0], rows.at[0, OWN, :, k], along_z(k)) for k in order[1:]
    }
    x_low, x_high, y_low, y_high, sib_own = {}, {}, {}, {}, {}
    for k in order:
        if k:
            from_z[k].wait_recv()
        low, high = rows.at[0, OWN, 0, k], rows.at[0, OWN, 1, k]
        x_low[k] = send(low, rows.at[0, FLIP_X, 0, k], across_x)
        y_high[k] = send(high, rows.at[0, FLIP_Y, 1, k], across_y)
        sib_own[k] = send(rows.at[0, OWN, :, k], rows.at[1, OWN, :, k], sibling)
        y_low[k] = send(low, rows.at[0, FLIP_Y, 0, k], across_y)
        x_high[k] = send(high, rows.at[0, FLIP_X, 1, k], across_x)
    far_low, far_high = {}, {}
    for k in order:
        x_low[k].wait_recv()
        far_low[k] = send(rows.at[0, FLIP_X, 0, k], rows.at[0, FLIP_BOTH, 0, k], across_y)
        y_high[k].wait_recv()
        far_high[k] = send(rows.at[0, FLIP_Y, 1, k], rows.at[0, FLIP_BOTH, 1, k], across_x)

    sib_half = {}

    def pass_on(place, part):
        sib_half[place, part] = send(
            rows.at[0, place, part], rows.at[1, place, part], sibling
        )

    pass_on(FLIP_X, 0)
    pass_on(FLIP_Y, 1)

    column_of = lax.broadcasted_iota(jnp.int32, (16, extra), 1) % expert_count
    wanted = ep * local + lax.broadcasted_iota(jnp.int32, (16, extra), 0)
    limit = (ep + 1) * local
    pick = jnp.where((column_of == wanted) & (wanted < limit), 1.0, 0.0).astype(jnp.bfloat16)
    above = lax.broadcasted_iota(jnp.int32, (chunk, chunk), 0)
    below = lax.broadcasted_iota(jnp.int32, (chunk, chunk), 1)
    earlier = jnp.where(
        (above < below) & ((above // half) % LINE == (below // half) % LINE), 1.0, 0.0
    ).astype(jnp.bfloat16)
    start_slot = (
        ((lax.broadcasted_iota(jnp.int32, (16, chunk), 1) // half) % LINE) * capacity
    ).astype(jnp.float32)
    slot_number = lax.broadcasted_iota(jnp.int32, (slots, chunk), 0).astype(jnp.float32)

    def place_rows(place):
        for plane in range(2):
            packed = rows[plane, place, :, :, :, width:].reshape(chunk, extra)
            weight = lax.dot_general(
                pick, packed, (((1,), (1,)), ((), ())), preferred_element_type=jnp.float32
            )
            mask = jnp.where(weight > 0, 1.0, 0.0)
            rank = jnp.dot(
                mask.astype(jnp.bfloat16), earlier, preferred_element_type=jnp.float32
            )
            target = jnp.where(mask > 0, start_slot + rank, -1.0)
            for e in range(local):
                hit = jnp.where(target[e : e + 1, :] == slot_number, 1.0, 0.0)
                placing[plane, e] = hit.astype(jnp.bfloat16)
                total = jnp.sum(hit * weight[e : e + 1, :], axis=1, keepdims=True)
                slot_weight[e, plane * slots : (plane + 1) * slots, :] = jnp.broadcast_to(
                    total, (slots, 128)
                )
            table = placing[plane].reshape(local * slots, chunk)

            @pl.loop(0, tiles)
            def _(t):
                span = pl.ds(pl.multiple_of(t * tile, tile), tile)
                piece = rows[plane, place, :, :, :, span].reshape(chunk, tile)
                found = jnp.dot(table, piece, preferred_element_type=jnp.float32)
                grouped[:, plane * slots : (plane + 1) * slots, span] = found.astype(
                    jnp.bfloat16
                ).reshape(local, slots, tile)

    def run_experts():
        @pl.loop(0, local)
        def _(e):
            batch = grouped[e]
            gate_proj = jnp.dot(batch, gate[e], preferred_element_type=jnp.float32)
            up_proj = jnp.dot(batch, up[e], preferred_element_type=jnp.float32)
            active = gate_proj / (1.0 + jnp.exp(-gate_proj)) * up_proj * slot_weight[e][:, :1]
            active = active.astype(jnp.bfloat16)
            for t in range(tiles):
                part = lax.dot_general(
                    active, down[e, t * tile : (t + 1) * tile, :], (((1,), (1,)), ((), ())),
                    preferred_element_type=jnp.float32,
                )
                grouped[e, :, t * tile : (t + 1) * tile] = part.astype(jnp.bfloat16)

    def combine(plane, place, target, added):
        table = placing[plane].reshape(local * slots, chunk)

        @pl.loop(0, tiles)
        def _(t):
            span = pl.ds(pl.multiple_of(t * tile, tile), tile)
            piece = grouped[:, plane * slots : (plane + 1) * slots, span]
            result = lax.dot_general(
                table, piece.reshape(local * slots, tile), (((0,), (0,)), ((), ())),
                preferred_element_type=jnp.float32,
            ).reshape(2, LINE, half, tile)
            if added is not None:
                result = result + added[place, :, :, :, span].astype(jnp.float32)
            target[place, :, :, :, span] = result.astype(jnp.bfloat16)

    def group(place):
        place_rows(place)
        run_experts()
        combine(1, place, sibling_share, None)
        copy = send(sibling_share.at[place], sibling_sum.at[place], sibling)
        copy.wait_recv()
        combine(0, place, share, sibling_sum)

    for k in order:
        sib_own[k].wait_recv()
    for copy in weight_copies:
        copy.wait()
    group(OWN)

    for k in order:
        x_high[k].wait_recv()
        y_low[k].wait_recv()
    pass_on(FLIP_X, 1)
    pass_on(FLIP_Y, 0)
    for k in order:
        far_low[k].wait_recv()
        far_high[k].wait_recv()
    pass_on(FLIP_BOTH, 0)
    pass_on(FLIP_BOTH, 1)

    for part in range(2):
        sib_half[FLIP_BOTH, part].wait_recv()
    group(FLIP_BOTH)
    y_first = send(share.at[FLIP_BOTH, 0], first_y.at[0], across_y)
    x_first = send(share.at[FLIP_BOTH, 1], first_x.at[0], across_x)
    for part in range(2):
        sib_half[FLIP_X, part].wait_recv()
    group(FLIP_X)
    x_next = send(share.at[FLIP_X, 1], first_x.at[1], across_x)
    for part in range(2):
        sib_half[FLIP_Y, part].wait_recv()
    group(FLIP_Y)
    y_next = send(share.at[FLIP_Y, 0], first_y.at[1], across_y)

    def add_into(target, terms):
        for k in range(LINE):
            total = terms[0][k].astype(jnp.float32)
            for term in terms[1:]:
                total = total + term[k].astype(jnp.float32)
            target[k] = total.astype(jnp.bfloat16)

    y_first.wait_recv()
    low_sum = share.at[FLIP_X, 0]
    add_into(low_sum, (low_sum, first_y.at[0]))
    x_last = send(low_sum, second_x, across_x)
    x_first.wait_recv()
    high_sum = share.at[FLIP_Y, 1]
    add_into(high_sum, (high_sum, first_x.at[0]))
    y_last = send(high_sum, second_y, across_y)
    x_next.wait_recv()
    y_next.wait_recv()
    x_last.wait_recv()
    add_into(column.at[0], (share.at[OWN, 0], first_y.at[1], second_x))
    y_last.wait_recv()
    add_into(column.at[1], (share.at[OWN, 1], first_x.at[1], second_y))
    ends = [
        send(column.at[:, k], last.at[k - 1], along_z(LINE - k)) for k in (1, 3, 2)
    ]
    for copy in ends:
        copy.wait_recv()
    gain = gain_ref[...].astype(jnp.float32)
    for part in range(2):
        total = column[part, 0].astype(jnp.float32)
        for k in range(LINE - 1):
            total = total + last[k, part].astype(jnp.float32)
        total = total + mixed_ref[part * half : (part + 1) * half]
        mean_square = jnp.mean(total * total, axis=-1, keepdims=True)
        out_ref[part * half : (part + 1) * half] = (
            total * lax.rsqrt(mean_square + epsilon) * gain
        ).astype(jnp.bfloat16)
    for copy in started:
        copy.wait_send()


COPIES = 50


def boxed(
    context, residual, out_proj, attn_gain, router, expert_ids,
    gate_weight, up_weight, down_weight, final_gain,
):
    row_count, width = context.shape
    mixed_stream, normed, weights = front(
        context, residual, out_proj, attn_gain, router, expert_ids
    )
    top = weights.astype(jnp.bfloat16)
    rest = (weights - top.astype(jnp.float32)).astype(jnp.bfloat16)
    block = jnp.concatenate([normed, top, rest], axis=1)
    half = row_count // 2
    local = gate_weight.shape[0]
    slots = LINE * capacity
    chunk = 2 * LINE * half
    low = jnp.bfloat16
    vmem = pl.BlockSpec(memory_space=pltpu.VMEM)
    hbm = pl.BlockSpec(memory_space=pl.ANY)
    return pl.pallas_call(
        box_kernel,
        out_shape=jax.ShapeDtypeStruct((row_count, width), low),
        in_specs=[vmem, vmem, vmem, hbm, hbm, hbm],
        out_specs=vmem,
        scratch_shapes=[
            pltpu.VMEM((2, 4, 2, LINE, half, block.shape[1]), low),
            pltpu.VMEM(gate_weight.shape, low),
            pltpu.VMEM(up_weight.shape, low),
            pltpu.VMEM(down_weight.shape, low),
            pltpu.VMEM((local, 2 * slots, width), low),
            pltpu.VMEM((2, local, slots, chunk), low),
            pltpu.VMEM((local, 2 * slots, 128), jnp.float32),
            pltpu.VMEM((4, 2, LINE, half, width), low),
            pltpu.VMEM((4, 2, LINE, half, width), low),
            pltpu.VMEM((4, 2, LINE, half, width), low),
            pltpu.VMEM((2, LINE, half, width), low),
            pltpu.VMEM((2, LINE, half, width), low),
            pltpu.VMEM((LINE, half, width), low),
            pltpu.VMEM((LINE, half, width), low),
            pltpu.VMEM((2, LINE, half, width), low),
            pltpu.VMEM((LINE - 1, 2, half, width), low),
            pltpu.SemaphoreType.DMA((3,)),
            pltpu.SemaphoreType.DMA((COPIES,)),
            pltpu.SemaphoreType.DMA((COPIES,)),
        ],
        compiler_params=pltpu.CompilerParams(
            collective_id=0, has_side_effects=True, vmem_limit_bytes=63 * 1024 * 1024
        ),
    )(block, mixed_stream, final_gain.reshape(1, width), gate_weight, up_weight, down_weight)


def solution(mesh):
    per_device = boxed if dict(mesh.shape) == {"ep": 2 * LINE, "rep": 4} else gathered
    in_specs = (
        P(("ep", "rep"), None),
        P(("ep", "rep"), None),
        P(),
        P(),
        P(),
        P(("ep", "rep"), None),
        P("ep", None, "rep"),
        P("ep", None, "rep"),
        P("ep", None, "rep"),
        P(),
    )
    out_specs = P(("ep", "rep"), None)
    return jax.shard_map(
        per_device, mesh=mesh, in_specs=in_specs, out_specs=out_specs, check_vma=False
    )
```

```python
import jax
import jax.numpy as jnp
from jax import lax
from jax.experimental import pallas as pl
from jax.experimental.pallas import tpu as pltpu
from jax.sharding import PartitionSpec as P

epsilon = 1e-05
capacity = 16


def rms_scale(values, gain_vector):
    mean_square = jnp.mean(values * values, axis=-1, keepdims=True)
    return values * lax.rsqrt(mean_square + epsilon) * gain_vector.astype(jnp.float32)


def front(context, residual, out_proj, attn_gain, router, expert_ids):
    expert_count = router.shape[1]
    attention = jnp.dot(context, out_proj, preferred_element_type=jnp.float32)
    mixed_stream = residual.astype(jnp.float32) + attention
    normed = rms_scale(mixed_stream, attn_gain).astype(jnp.bfloat16)
    logits = jnp.dot(normed, router, preferred_element_type=jnp.float32)
    probs = jax.nn.softmax(logits, axis=1)
    chosen = jnp.any(
        expert_ids[:, :, None] == jnp.arange(expert_count, dtype=jnp.int32)[None, None, :], axis=1
    )
    weights = jnp.where(chosen, probs, 0.0)
    return mixed_stream, normed, weights


def gathered(
    context, residual, out_proj, attn_gain, router, expert_ids,
    gate_weight, up_weight, down_weight, final_gain,
):
    row_count, model_width = context.shape
    local_experts = gate_weight.shape[0]
    owners = lax.axis_size("ep")
    sources = owners * lax.axis_size("rep")
    mixed_stream, normed, weights = front(
        context, residual, out_proj, attn_gain, router, expert_ids
    )
    high = weights.astype(jnp.bfloat16)
    low = (weights - high.astype(jnp.float32)).astype(jnp.bfloat16)
    block = jnp.concatenate([normed, high, low], axis=1)
    everyone = lax.all_gather(block, ("ep", "rep"), axis=0, tiled=False)
    rows = everyone[:, :, :model_width]
    first = model_width + lax.axis_index("ep") * local_experts
    high = lax.dynamic_slice_in_dim(everyone, first, local_experts, axis=2)
    low = lax.dynamic_slice_in_dim(everyone, first + weights.shape[1], local_experts, axis=2)
    local_weights = high.astype(jnp.float32) + low.astype(jnp.float32)
    mask = (local_weights > 0).astype(jnp.float32)
    earlier = (
        jnp.arange(row_count)[:, None] > jnp.arange(row_count)[None, :]
    ).astype(jnp.float32)
    rank = jnp.einsum("ij,sje->sie", earlier, mask)
    slots = jnp.arange(capacity, dtype=jnp.float32)
    placing = jnp.where(
        (rank[:, :, :, None] == slots) & (mask[:, :, :, None] > 0), 1.0, 0.0
    )
    slot_weight = jnp.sum(placing * local_weights[:, :, :, None], axis=1)
    placing = placing.astype(jnp.bfloat16).reshape(sources, row_count, local_experts * capacity)
    grouped = jnp.einsum(
        "sit,sid->std", placing, rows, preferred_element_type=jnp.float32
    ).astype(jnp.bfloat16)
    grouped = grouped.reshape(sources, local_experts, capacity, model_width)
    gate_proj = jnp.einsum(
        "serd,edw->serw", grouped, gate_weight, preferred_element_type=jnp.float32
    )
    up_proj = jnp.einsum("serd,edw->serw", grouped, up_weight, preferred_element_type=jnp.float32)
    active = (jax.nn.silu(gate_proj) * up_proj * slot_weight[..., None]).astype(jnp.bfloat16)
    part = jnp.einsum(
        "serw,edw->serd", active, down_weight, preferred_element_type=jnp.float32
    ).astype(jnp.bfloat16)
    part = part.reshape(sources, local_experts * capacity, model_width)
    share = jnp.einsum("sit,std->sid", placing, part, preferred_element_type=jnp.float32)
    share = share.astype(jnp.bfloat16).reshape(sources * row_count, model_width)
    expert_mix = lax.psum_scatter(share, ("ep", "rep"), scatter_dimension=0, tiled=True)
    total = mixed_stream + expert_mix.astype(jnp.float32)
    return rms_scale(total, final_gain).astype(jnp.bfloat16)


MESH = pl.DeviceIdType.MESH
LINE = 4
OWN, FLIP_Y, FLIP_X, FLIP_BOTH = 0, 1, 2, 3


def box_kernel(
    block_ref, mixed_ref, gain_ref, gate_hbm, up_hbm, down_hbm, out_ref,
    rows, gate, up, down, grouped, placing, slot_weight,
    sibling_share, sibling_sum, share, first_x, first_y, second_x, second_y, column, last,
    weight_sem, send_sem, recv_sem,
):
    half = block_ref.shape[0] // 2
    width = mixed_ref.shape[1]
    extra = block_ref.shape[1] - width
    expert_count = extra // 2
    local = gate.shape[0]
    chunk = 2 * LINE * half
    slots = LINE * capacity
    tile = 512
    tiles = width // tile

    ep, rep = lax.axis_index("ep"), lax.axis_index("rep")
    z, x, y, core = ep // 2, ep % 2, rep // 2, rep % 2
    across_x = (z * 2 + (1 - x), rep)
    across_y = (ep, (1 - y) * 2 + core)
    sibling = (ep, y * 2 + (1 - core))

    def along_z(step):
        return (((z + step) % LINE) * 2 + x, rep)

    peers = [across_x, across_y, sibling] + [along_z(step) for step in (1, 2, 3)]
    barrier = pltpu.get_barrier_semaphore()
    for peer in peers:
        pl.semaphore_signal(barrier, inc=1, device_id=peer, device_id_type=MESH)
    weight_copies = [
        pltpu.make_async_copy(source, target, weight_sem.at[i])
        for i, (source, target) in enumerate(((gate_hbm, gate), (up_hbm, up), (down_hbm, down)))
    ]
    for copy in weight_copies:
        copy.start()
    pl.semaphore_wait(barrier, len(peers))

    started = []

    def send(source, target, device):
        index = len(started)
        copy = pltpu.make_async_remote_copy(
            src_ref=source, dst_ref=target, send_sem=send_sem.at[index],
            recv_sem=recv_sem.at[index], device_id=device, device_id_type=MESH,
        )
        copy.start()
        started.append(copy)
        return copy

    rows[0, OWN, 0, 0] = block_ref[:half]
    rows[0, OWN, 1, 0] = block_ref[half:]
    order = (0, 1, 3, 2)
    from_z = {
        k: send(rows.at[0, OWN, :, 0], rows.at[0, OWN, :, k], along_z(k)) for k in order[1:]
    }
    x_low, x_high, y_low, y_high, sib_own = {}, {}, {}, {}, {}
    for k in order:
        if k:
            from_z[k].wait_recv()
        low, high = rows.at[0, OWN, 0, k], rows.at[0, OWN, 1, k]
        x_low[k] = send(low, rows.at[0, FLIP_X, 0, k], across_x)
        y_high[k] = send(high, rows.at[0, FLIP_Y, 1, k], across_y)
        sib_own[k] = send(rows.at[0, OWN, :, k], rows.at[1, OWN, :, k], sibling)
        y_low[k] = send(low, rows.at[0, FLIP_Y, 0, k], across_y)
        x_high[k] = send(high, rows.at[0, FLIP_X, 1, k], across_x)
    far_low, far_high = {}, {}

    def forward(k):
        x_low[k].wait_recv()
        far_low[k] = send(rows.at[0, FLIP_X, 0, k], rows.at[0, FLIP_BOTH, 0, k], across_y)
        y_high[k].wait_recv()
        far_high[k] = send(rows.at[0, FLIP_Y, 1, k], rows.at[0, FLIP_BOTH, 1, k], across_x)

    for k in order[:2]:
        forward(k)
    sib_half = {}

    def pass_on(place, part):
        sib_half[place, part] = send(
            rows.at[0, place, part], rows.at[1, place, part], sibling
        )

    column_of = lax.broadcasted_iota(jnp.int32, (16, extra), 1) % expert_count
    wanted = ep * local + lax.broadcasted_iota(jnp.int32, (16, extra), 0)
    limit = (ep + 1) * local
    pick = jnp.where((column_of == wanted) & (wanted < limit), 1.0, 0.0).astype(jnp.bfloat16)
    above = lax.broadcasted_iota(jnp.int32, (chunk, chunk), 0)
    below = lax.broadcasted_iota(jnp.int32, (chunk, chunk), 1)
    earlier = jnp.where(
        (above < below) & ((above // half) % LINE == (below // half) % LINE), 1.0, 0.0
    ).astype(jnp.bfloat16)
    start_slot = (
        ((lax.broadcasted_iota(jnp.int32, (16, chunk), 1) // half) % LINE) * capacity
    ).astype(jnp.float32)
    slot_number = lax.broadcasted_iota(jnp.int32, (slots, chunk), 0).astype(jnp.float32)

    def place_rows(place):
        for plane in range(2):
            packed = rows[plane, place, :, :, :, width:].reshape(chunk, extra)
            weight = lax.dot_general(
                pick, packed, (((1,), (1,)), ((), ())), preferred_element_type=jnp.float32
            )
            mask = jnp.where(weight > 0, 1.0, 0.0)
            rank = jnp.dot(
                mask.astype(jnp.bfloat16), earlier, preferred_element_type=jnp.float32
            )
            target = jnp.where(mask > 0, start_slot + rank, -1.0)
            for e in range(local):
                hit = jnp.where(target[e : e + 1, :] == slot_number, 1.0, 0.0)
                placing[plane, e] = hit.astype(jnp.bfloat16)
                total = jnp.sum(hit * weight[e : e + 1, :], axis=1, keepdims=True)
                slot_weight[e, plane * slots : (plane + 1) * slots, :] = jnp.broadcast_to(
                    total, (slots, 128)
                )
            table = placing[plane].reshape(local * slots, chunk)

            @pl.loop(0, tiles)
            def _(t):
                span = pl.ds(pl.multiple_of(t * tile, tile), tile)
                piece = rows[plane, place, :, :, :, span].reshape(chunk, tile)
                found = jnp.dot(table, piece, preferred_element_type=jnp.float32)
                grouped[:, plane * slots : (plane + 1) * slots, span] = found.astype(
                    jnp.bfloat16
                ).reshape(local, slots, tile)

    def run_experts():
        @pl.loop(0, local)
        def _(e):
            batch = grouped[e]
            gate_proj = jnp.dot(batch, gate[e], preferred_element_type=jnp.float32)
            up_proj = jnp.dot(batch, up[e], preferred_element_type=jnp.float32)
            active = gate_proj / (1.0 + jnp.exp(-gate_proj)) * up_proj * slot_weight[e][:, :1]
            active = active.astype(jnp.bfloat16)
            for t in range(tiles):
                part = lax.dot_general(
                    active, down[e, t * tile : (t + 1) * tile, :], (((1,), (1,)), ((), ())),
                    preferred_element_type=jnp.float32,
                )
                grouped[e, :, t * tile : (t + 1) * tile] = part.astype(jnp.bfloat16)

    def combine(plane, place, target, added, first_tile):
        table = placing[plane].reshape(local * slots, chunk)

        @pl.loop(first_tile, first_tile + tiles // 2)
        def _(t):
            span = pl.ds(pl.multiple_of(t * tile, tile), tile)
            piece = grouped[:, plane * slots : (plane + 1) * slots, span]
            result = lax.dot_general(
                table, piece.reshape(local * slots, tile), (((0,), (0,)), ((), ())),
                preferred_element_type=jnp.float32,
            ).reshape(2, LINE, half, tile)
            if added is not None:
                result = result + added[place, :, :, :, span].astype(jnp.float32)
            target[place, :, :, :, span] = result.astype(jnp.bfloat16)

    def group(place, reduced):
        place_rows(place)
        run_experts()
        copies = []
        for first_tile in (0, tiles // 2):
            combine(1, place, sibling_share, None, first_tile)
            span = pl.ds(first_tile * tile, tiles // 2 * tile)
            copies.append(
                send(
                    sibling_share.at[place, :, :, :, span],
                    sibling_sum.at[place, :, :, :, span],
                    sibling,
                )
            )
        for first_tile, copy in zip((0, tiles // 2), copies):
            if reduced:
                copy.wait_recv()
            combine(0, place, share, sibling_sum if reduced else None, first_tile)
        return copies

    def send_each(source, target, device):
        return {k: send(source.at[k], target.at[k], device) for k in late}

    late = (2, 1, 3, 0)
    for k in order:
        sib_own[k].wait_recv()
    for copy in weight_copies:
        copy.wait()
    own_copies = group(OWN, False)

    for k in order[2:]:
        forward(k)
    for k in order:
        x_high[k].wait_recv()
    pass_on(FLIP_X, 0)
    pass_on(FLIP_X, 1)
    for k in order:
        y_low[k].wait_recv()
    pass_on(FLIP_Y, 0)
    pass_on(FLIP_Y, 1)
    for part in range(2):
        sib_half[FLIP_X, part].wait_recv()
    group(FLIP_X, True)
    x_next = send_each(share.at[FLIP_X, 1], first_x.at[1], across_x)
    for k in order:
        far_low[k].wait_recv()
        far_high[k].wait_recv()
    pass_on(FLIP_BOTH, 0)
    pass_on(FLIP_BOTH, 1)
    for part in range(2):
        sib_half[FLIP_Y, part].wait_recv()
    group(FLIP_Y, True)
    y_next = send_each(share.at[FLIP_Y, 0], first_y.at[1], across_y)
    for part in range(2):
        sib_half[FLIP_BOTH, part].wait_recv()
    group(FLIP_BOTH, True)
    y_first, x_first = {}, {}
    for k in late:
        y_first[k] = send(share.at[FLIP_BOTH, 0, k], first_y.at[0, k], across_y)
        x_first[k] = send(share.at[FLIP_BOTH, 1, k], first_x.at[0, k], across_x)
    for copy in own_copies:
        copy.wait_recv()

    def add_into(target, terms):
        total = terms[0][...].astype(jnp.float32)
        for term in terms[1:]:
            total = total + term[...].astype(jnp.float32)
        target[...] = total.astype(jnp.bfloat16)

    x_last, y_last, ends = {}, {}, {}

    def turn(k):
        y_first[k].wait_recv()
        low_sum = share.at[FLIP_X, 0, k]
        add_into(low_sum, (low_sum, first_y.at[0, k]))
        x_last[k] = send(low_sum, second_x.at[k], across_x)
        x_first[k].wait_recv()
        high_sum = share.at[FLIP_Y, 1, k]
        add_into(high_sum, (high_sum, first_x.at[0, k]))
        y_last[k] = send(high_sum, second_y.at[k], across_y)

    def finish(k):
        y_next[k].wait_recv()
        x_last[k].wait_recv()
        add_into(
            column.at[0, k],
            (share.at[OWN, 0, k], sibling_sum.at[OWN, 0, k], first_y.at[1, k], second_x.at[k]),
        )
        x_next[k].wait_recv()
        y_last[k].wait_recv()
        add_into(
            column.at[1, k],
            (share.at[OWN, 1, k], sibling_sum.at[OWN, 1, k], first_x.at[1, k], second_y.at[k]),
        )
        if k:
            ends[k] = send(column.at[:, k], last.at[k - 1], along_z(LINE - k))

    turn(late[0])
    turn(late[1])
    for i, k in enumerate(late):
        finish(k)
        if i + 2 < LINE:
            turn(late[i + 2])
    for copy in ends.values():
        copy.wait_recv()
    assert len(started) == COPIES, len(started)
    gain = gain_ref[...].astype(jnp.float32)
    for part in range(2):
        total = column[part, 0].astype(jnp.float32)
        for k in range(LINE - 1):
            total = total + last[k, part].astype(jnp.float32)
        total = total + mixed_ref[part * half : (part + 1) * half]
        mean_square = jnp.mean(total * total, axis=-1, keepdims=True)
        out_ref[part * half : (part + 1) * half] = (
            total * lax.rsqrt(mean_square + epsilon) * gain
        ).astype(jnp.bfloat16)
    for copy in started:
        copy.wait_send()


COPIES = 72


def boxed(
    context, residual, out_proj, attn_gain, router, expert_ids,
    gate_weight, up_weight, down_weight, final_gain,
):
    row_count, width = context.shape
    mixed_stream, normed, weights = front(
        context, residual, out_proj, attn_gain, router, expert_ids
    )
    top = weights.astype(jnp.bfloat16)
    rest = (weights - top.astype(jnp.float32)).astype(jnp.bfloat16)
    block = jnp.concatenate([normed, top, rest], axis=1)
    half = row_count // 2
    local = gate_weight.shape[0]
    slots = LINE * capacity
    chunk = 2 * LINE * half
    low = jnp.bfloat16
    vmem = pl.BlockSpec(memory_space=pltpu.VMEM)
    hbm = pl.BlockSpec(memory_space=pl.ANY)
    return pl.pallas_call(
        box_kernel,
        out_shape=jax.ShapeDtypeStruct((row_count, width), low),
        in_specs=[vmem, vmem, vmem, hbm, hbm, hbm],
        out_specs=vmem,
        scratch_shapes=[
            pltpu.VMEM((2, 4, 2, LINE, half, block.shape[1]), low),
            pltpu.VMEM(gate_weight.shape, low),
            pltpu.VMEM(up_weight.shape, low),
            pltpu.VMEM(down_weight.shape, low),
            pltpu.VMEM((local, 2 * slots, width), low),
            pltpu.VMEM((2, local, slots, chunk), low),
            pltpu.VMEM((local, 2 * slots, 128), jnp.float32),
            pltpu.VMEM((4, 2, LINE, half, width), low),
            pltpu.VMEM((4, 2, LINE, half, width), low),
            pltpu.VMEM((4, 2, LINE, half, width), low),
            pltpu.VMEM((2, LINE, half, width), low),
            pltpu.VMEM((2, LINE, half, width), low),
            pltpu.VMEM((LINE, half, width), low),
            pltpu.VMEM((LINE, half, width), low),
            pltpu.VMEM((2, LINE, half, width), low),
            pltpu.VMEM((LINE - 1, 2, half, width), low),
            pltpu.SemaphoreType.DMA((3,)),
            pltpu.SemaphoreType.DMA((COPIES,)),
            pltpu.SemaphoreType.DMA((COPIES,)),
        ],
        compiler_params=pltpu.CompilerParams(
            collective_id=0, has_side_effects=True, vmem_limit_bytes=63 * 1024 * 1024
        ),
    )(block, mixed_stream, final_gain.reshape(1, width), gate_weight, up_weight, down_weight)


def solution(mesh):
    per_device = boxed if dict(mesh.shape) == {"ep": 2 * LINE, "rep": 4} else gathered
    in_specs = (
        P(("ep", "rep"), None),
        P(("ep", "rep"), None),
        P(),
        P(),
        P(),
        P(("ep", "rep"), None),
        P("ep", None, "rep"),
        P("ep", None, "rep"),
        P("ep", None, "rep"),
        P(),
    )
    out_specs = P(("ep", "rep"), None)
    return jax.shard_map(
        per_device, mesh=mesh, in_specs=in_specs, out_specs=out_specs, check_vma=False
    )
```
